32 devices in a mesh: ens: 2 (over y), space: 16 (over z, x, core).
Axes of the slice: x: 2, y: 2, z: 4, core: 2. Of those that a mesh axis runs over, the one named last changes fastest.
Arguments:
- node_states: bfloat16 [2, 2048, 1024], P('ens', 'space'), may hold values from -6 to 6
- query: bfloat16 [2, 2048, 512], P('ens', 'space'), may hold values from -240 to 240
- key: bfloat16 [2, 2048, 512], P('ens', 'space'), may hold values from -6 to 6
- value: bfloat16 [2, 2048, 512], P('ens', 'space'), may hold values from -6 to 6
- out_weight: bfloat16 [512, 1024], replicated, may hold values from -0.25 to 0.25
- dec_weight: bfloat16 [100, 1024], replicated, may hold values from -0.1875 to 0.1875
- target: float32 [100, 16384], P(None, 'space'), may hold values from -6 to 6
- area_weight: float32 [16384], P('space'), may hold values from 0.25 to 2.5
- var_weight: float32 [100], replicated, may hold values from 0.5 to 5
- edges: int32 [3, 16384], P(None, 'space'), may hold values from 0 to 2047, as said below
- edge_weight: float32 [3, 16384], P(None, 'space'), may hold values from 0.1 to 0.6
- windows: int32 [2, 16], P(None, 'space'), may hold values from 0 to 2048, as said below
Outputs:
- grad_states: bfloat16 [2, 2048, 1024], P('ens', 'space')
- grad_query: bfloat16 [2, 2048, 512], P('ens', 'space')
- grad_key: bfloat16 [2, 2048, 512], P('ens', 'space')
- grad_value: bfloat16 [2, 2048, 512], P('ens', 'space')
- grad_wo: float32 [512, 1024], P('space')
- grad_dec: float32 [100, 1024], replicated
The draws below stay inside these ranges and needn't reach their ends.
Inputs may be any that keep to these rules, and one draw needn't show every extreme that they name: The edges of a point among the 1024 points p with p // 1024 = d name nodes from d * 128 - 128 to d * 128 + 2 * 128 - 1; both ends are named in every draw. For the block b of nodes s = b * 128 to s + 127: max(0, s - 128) <= windows[0, b] <= s and s + 128 <= windows[1, b] <= min(2048, s + 256); the outer ends s - 128 and s + 256 are reached by some block in every draw.
All inputs are finite; a program needn't handle non-finite values.
Results may differ from the reference program's by a relative error of at most 0.017.
Values may be sent and summed in bfloat16 or wider, within the bound.
A program may use at most 64 MiB of HBM per device.

```python
import math
import jax
import jax.numpy as jnp
from jax import lax

D = 1024
V = 100
HEADS = 8
HEAD_DIM = 64
KNB = 3
BLOCK = 128
NODE_DEV = 128
PT_DEV = 1024
ATT = 512
MEMBERS = 2
NODES = 2048
POINTS = 16384
N_SPACE = 16


def query_key_pair(key):
    base_key = jax.random.fold_in(key, 17)
    query_seed, key_seed = jax.random.split(base_key, 2)
    shape_full = (MEMBERS, NODES, ATT)
    queries = jnp.clip(jax.random.normal(query_seed, shape_full, jnp.float32), -6.0, 6.0)
    keys_drawn = jnp.clip(jax.random.normal(key_seed, shape_full, jnp.float32), -6.0, 6.0)
    return (queries, keys_drawn)


def draw_query(key, part):
    return query_key_pair(key)[0].astype(jnp.bfloat16)


def draw_key(key, part):
    return query_key_pair(key)[1].astype(jnp.bfloat16)


def draw_edges(key, part):
    offset_seed, low_seed, high_seed = jax.random.split(jax.random.fold_in(key, 29), 3)
    point_ids = jnp.arange(POINTS)
    band_ids = point_ids // PT_DEV
    base_node = band_ids * NODE_DEV + point_ids % PT_DEV * NODE_DEV // PT_DEV
    offsets = jax.random.randint(offset_seed, (KNB, POINTS), -NODE_DEV, NODE_DEV)
    node_ids = base_node[None, :] + offsets
    low_band = jax.random.randint(low_seed, (), 1, N_SPACE)
    high_band = jax.random.randint(high_seed, (), 0, N_SPACE - 1)
    slot_ids = jnp.arange(KNB)[:, None]
    lowest_spot = (point_ids[None, :] == low_band * PT_DEV) & (slot_ids == 0)
    highest_spot = (point_ids[None, :] == high_band * PT_DEV + PT_DEV - 1) & (slot_ids == 0)
    node_ids = jnp.where(lowest_spot, low_band * NODE_DEV - NODE_DEV, node_ids)
    node_ids = jnp.where(highest_spot, high_band * NODE_DEV + 2 * NODE_DEV - 1, node_ids)
    return jnp.clip(node_ids, 0, NODES - 1).astype(jnp.int32)


def draw_windows(key, part):
    back_seed, ahead_seed, first_seed, last_seed = jax.random.split(jax.random.fold_in(key, 41), 4)
    block_count = NODES // BLOCK
    per_band = NODE_DEV // BLOCK
    block_ids = jnp.arange(block_count)
    reach_back = jax.random.randint(back_seed, (block_count,), NODE_DEV // 4, NODE_DEV + 1)
    reach_ahead = jax.random.randint(ahead_seed, (block_count,), NODE_DEV // 4, NODE_DEV + 1)
    first_pick = jax.random.randint(first_seed, (), 1, N_SPACE) * per_band
    last_pick = jax.random.randint(last_seed, (), 0, N_SPACE - 1) * per_band + per_band - 1
    reach_back = jnp.where(block_ids == first_pick, NODE_DEV, reach_back)
    reach_ahead = jnp.where(block_ids == last_pick, NODE_DEV, reach_ahead)
    block_start = block_ids * BLOCK
    lower_end = jnp.maximum(block_start - reach_back, 0)
    upper_end = jnp.minimum(block_start + BLOCK + reach_ahead, NODES)
    return jnp.stack([lower_end, upper_end]).astype(jnp.int32)


def block_scale(stream_key, dims, pieces, low, largest):
    level, own = 1.0, jax.random.fold_in(stream_key, 6)
    for axis_at, blocks in pieces:
        steps = jnp.exp(jax.random.uniform(jax.random.fold_in(own, axis_at), (blocks,), jnp.float32, low / len(pieces), largest / len(pieces)))
        level = level * jnp.repeat(steps, dims[axis_at] // blocks).reshape([-1 if axis == axis_at else 1 for axis in range(len(dims))])
    return level


def normal_values(rng, dims, deviation, reach, shards=(), kind=jnp.bfloat16):
    loudness = block_scale(rng, dims, shards, -0.22, 0.18) if shards else 1.0
    entries = jax.random.normal(rng, dims, jnp.float32) * deviation * loudness
    return jnp.minimum(jnp.maximum(entries, -reach), reach).astype(kind)


def setup_inputs(seed: int = 0) -> dict:
    streams_of = jax.random.split(jax.random.key(seed), 13)
    node_states = normal_values(streams_of[0], (MEMBERS, NODES, D), 1.0, 6.0, ((0, 2), (1, 16)))
    query = draw_query(jax.random.fold_in(streams_of[12], 71), 0)
    key = draw_key(jax.random.fold_in(streams_of[12], 71), 0)
    value = normal_values(streams_of[3], (MEMBERS, NODES, ATT), 1.0, 6.0, ((0, 2), (1, 16)))
    out_weight = normal_values(streams_of[4], (ATT, D), ATT ** -0.5, 0.25)
    dec_weight = normal_values(streams_of[5], (V, D), D ** -0.5, 0.1875)
    target = normal_values(streams_of[6], (V, POINTS), 1.0, 6.0, ((1, 16),), jnp.float32)
    area_weight = jnp.clip(jnp.exp(math.log(2.5) - 2.3025851 * jax.random.uniform(streams_of[7], (POINTS,), jnp.float32) ** block_scale(streams_of[7], (POINTS,), ((0, 16),), -0.2, 0.2)), 0.25, 2.5)
    var_weight = jnp.clip(jnp.exp(jax.random.uniform(streams_of[8], (V,), jnp.float32, math.log(0.5), math.log(5.0))), 0.5, 5.0)
    edges = draw_edges(jax.random.fold_in(streams_of[12], 71), 0)
    edge_weight = jnp.clip(0.1 + 0.5 * jax.random.uniform(streams_of[10], (KNB, POINTS), jnp.float32) ** block_scale(streams_of[10], (KNB, POINTS), ((1, 16),), -0.2, 0.2), 0.1, 0.6)
    windows = draw_windows(jax.random.fold_in(streams_of[12], 71), 0)
    return dict(node_states=node_states, query=query, key=key, value=value, out_weight=out_weight, dec_weight=dec_weight, target=target, area_weight=area_weight, var_weight=var_weight, edges=edges, edge_weight=edge_weight, windows=windows)


SMOOTH_SQUARE = 0.0625
MASKED_SCORE = -1e+30

def smooth_slope(diff_value):
    return diff_value * lax.rsqrt(diff_value * diff_value + SMOOTH_SQUARE)

def decode(states, edges, edge_weight):
    latent_sum = jnp.zeros((edges.shape[1], states.shape[1]), jnp.float32)
    for edge_slot in range(edges.shape[0]):
        latent_sum = latent_sum + edge_weight[edge_slot][:, None] * jnp.take(states, edges[edge_slot], axis=0).astype(jnp.float32)
    return latent_sum.astype(jnp.bfloat16)

def attention_grads(query, key, value, grad_states, out_weight, windows):
    node_count = query.shape[0]
    key_span = BLOCK + 2 * NODE_DEV
    padding = ((NODE_DEV, NODE_DEV), (0, 0))
    key_pad = jnp.pad(key, padding)
    value_pad = jnp.pad(value, padding)
    grad_out = jnp.dot(grad_states, out_weight.T, preferred_element_type=jnp.float32).astype(jnp.bfloat16)
    score_scale = 1.0 / math.sqrt(HEAD_DIM)

    def one_block(totals, block_index):
        key_grads, value_grads = totals
        first_row = block_index * BLOCK
        query_heads = lax.dynamic_slice_in_dim(query, first_row, BLOCK, 0).astype(jnp.float32).reshape(BLOCK, HEADS, HEAD_DIM)
        key_heads = lax.dynamic_slice_in_dim(key_pad, first_row, key_span, 0).astype(jnp.float32).reshape(key_span, HEADS, HEAD_DIM)
        value_heads = lax.dynamic_slice_in_dim(value_pad, first_row, key_span, 0).astype(jnp.float32).reshape(key_span, HEADS, HEAD_DIM)
        grad_heads = lax.dynamic_slice_in_dim(grad_out, first_row, BLOCK, 0).astype(jnp.float32).reshape(BLOCK, HEADS, HEAD_DIM)
        key_place = first_row - NODE_DEV + jnp.arange(key_span, dtype=jnp.int32)
        inside = (key_place >= windows[0, block_index]) & (key_place < windows[1, block_index])
        scores = jnp.einsum('qhc,khc->hqk', query_heads, key_heads) * score_scale
        scores = jnp.where(inside[None, None, :], scores, MASKED_SCORE)
        row_max = lax.optimization_barrier(jnp.max(scores, axis=-1, keepdims=True))
        exponent = jnp.exp(scores - row_max)
        attn_prob = exponent / lax.optimization_barrier(jnp.sum(exponent, axis=-1, keepdims=True))
        prob_low = lax.optimization_barrier(attn_prob.astype(jnp.bfloat16)).astype(jnp.float32)
        attn_rows = jnp.einsum('hqk,khc->qhc', prob_low, value_heads).reshape(BLOCK, -1).astype(jnp.bfloat16)
        value_term = jnp.einsum('hqk,qhc->khc', prob_low, grad_heads).reshape(key_span, -1)
        grad_prob = jnp.einsum('qhc,khc->hqk', grad_heads, value_heads)
        row_delta = lax.optimization_barrier(jnp.sum(attn_prob * grad_prob, axis=-1, keepdims=True))
        grad_scores = lax.optimization_barrier((attn_prob * (grad_prob - row_delta)).astype(jnp.bfloat16)).astype(jnp.float32)
        query_rows = (jnp.einsum('hqk,khc->qhc', grad_scores, key_heads) * score_scale).reshape(BLOCK, -1).astype(jnp.bfloat16)
        key_term = (jnp.einsum('hqk,qhc->khc', grad_scores, query_heads) * score_scale).reshape(key_span, -1)
        key_grads = lax.dynamic_update_slice_in_dim(key_grads, lax.dynamic_slice_in_dim(key_grads, first_row, key_span, 0) + key_term, first_row, 0)
        value_grads = lax.dynamic_update_slice_in_dim(value_grads, lax.dynamic_slice_in_dim(value_grads, first_row, key_span, 0) + value_term, first_row, 0)
        return ((key_grads, value_grads), (attn_rows, query_rows))
    zero_rows = jnp.zeros((node_count + 2 * NODE_DEV, query.shape[1]), jnp.float32)
    block_ids = jnp.arange(node_count // BLOCK, dtype=jnp.int32)
    (key_grads, value_grads), (attn_rows, query_rows) = lax.scan(one_block, (zero_rows, zero_rows), block_ids)
    attn_out = attn_rows.reshape(node_count, -1)
    grad_query = query_rows.reshape(node_count, -1)
    grad_key = key_grads[NODE_DEV:NODE_DEV + node_count].astype(jnp.bfloat16)
    grad_value = value_grads[NODE_DEV:NODE_DEV + node_count].astype(jnp.bfloat16)
    return (attn_out, grad_query, grad_key, grad_value)

def reference(node_states, query, key, value, out_weight, dec_weight, target, area_weight, var_weight, edges, edge_weight, windows):
    members = node_states.shape[0]

    def predict(states):
        latent = decode(states, edges, edge_weight)
        return lax.dot_general(dec_weight, latent, (((1,), (1,)), ((), ())), preferred_element_type=jnp.float32).astype(jnp.bfloat16)
    prediction = lax.map(predict, node_states)
    weights = area_weight[None, :] * var_weight[:, None]

    def member_grad(own_preds):
        own_values = own_preds.astype(jnp.float32)
        pair_sum = jnp.zeros_like(own_values)
        for other in range(members):
            pair_sum = pair_sum + smooth_slope(own_values - prediction[other].astype(jnp.float32))
        slopes = smooth_slope(own_values - target) - pair_sum / (members - 1)
        return (weights * slopes).astype(jnp.bfloat16)
    grad_prediction = lax.map(member_grad, prediction)

    def one_member(totals, inputs):
        wo_total, dec_total = totals
        states, member_grads, query_m, key_m, value_m = inputs
        latent = decode(states, edges, edge_weight)
        grad_latent = lax.dot_general(member_grads, dec_weight, (((0,), (0,)), ((), ())), preferred_element_type=jnp.float32)
        dec_total = dec_total + lax.dot_general(member_grads, latent, (((1,), (0,)), ((), ())), preferred_element_type=jnp.float32)
        node_sum = jnp.zeros((states.shape[0], states.shape[1]), jnp.float32)
        for edge_slot in range(edges.shape[0]):
            node_sum = node_sum.at[edges[edge_slot]].add(edge_weight[edge_slot][:, None] * grad_latent)
        grad_states = node_sum.astype(jnp.bfloat16)
        attn_out, grad_query, grad_key, grad_value = attention_grads(query_m, key_m, value_m, grad_states, out_weight, windows)
        wo_total = wo_total + lax.dot_general(attn_out, grad_states, (((0,), (0,)), ((), ())), preferred_element_type=jnp.float32)
        return ((wo_total, dec_total), (grad_states, grad_query, grad_key, grad_value))
    start_totals = (jnp.zeros((query.shape[2], node_states.shape[2]), jnp.float32), jnp.zeros((dec_weight.shape[0], dec_weight.shape[1]), jnp.float32))
    (grad_wo, grad_dec), (grad_states, grad_query, grad_key, grad_value) = lax.scan(one_member, start_totals, (node_states, grad_prediction, query, key, value))
    return (grad_states, grad_query, grad_key, grad_value, grad_wo, grad_dec)
```

```python
import functools
import math

import jax
import jax.numpy as jnp
from jax import lax
from jax.experimental import pallas as pl
from jax.experimental.pallas import tpu as pltpu
from jax.sharding import PartitionSpec as P

HEAD_DIM = 64
BLOCK = 128
INNER = 4
LANES = 128
SMOOTH_SQUARE = 0.0625
MASKED_SCORE = -1e30
F32 = jnp.float32
BF16 = jnp.bfloat16
NT = (((1,), (1,)), ((), ()))
TN = (((0,), (0,)), ((), ()))


def smooth_slope(diff_value):
    return diff_value * lax.rsqrt(diff_value * diff_value + SMOOTH_SQUARE)


def dot(a, b, dims=(((1,), (0,)), ((), ()))):
    return lax.dot_general(a, b, dims, preferred_element_type=F32)


def kernel(
    n_e,
    n_s,
    states_hbm,
    q_hbm,
    k_hbm,
    v_hbm,
    ow_hbm,
    dec_hbm,
    target_hbm,
    area_hbm,
    var_hbm,
    edges_hbm,
    ew_hbm,
    win_hbm,
    gs_ref,
    gq_ref,
    gk_ref,
    gv_ref,
    gwo_ref,
    gdec_ref,
    states_ref,
    q_ref,
    k_ref,
    v_ref,
    ow_ref,
    dec_ref,
    target_ref,
    area_ref,
    var_ref,
    edges_ref,
    ew_ref,
    win_ref,
    decp,
    mix,
    wt,
    kh,
    text,
    gp,
    qsend,
    qrecv,
    qs,
    prob,
    ao,
    go,
    kmid,
    vmid,
    bsend,
    brecv,
    csend,
    crecv,
    dsend,
    drecv,
    zsend,
    zrecv,
    fsend,
    frecv,
    agsend,
    dall,
    kv_s,
    kv_r,
    t_s,
    t_r,
    q_s,
    q_r,
    b_s,
    b_r,
    c_s,
    c_r,
    d_s,
    d_r,
    a_s,
    a_r,
    z_s,
    z_r,
    f_s,
    f_r,
    load_sem,
    hello_sem,
):
    e = lax.axis_index("ens")
    s = lax.axis_index("space")
    inner = math.gcd(n_s, INNER)
    outer = n_s // inner
    group = n_e * inner
    ring, seat = lax.div(s, inner), lax.rem(s, inner)
    mine = e * inner + seat
    nodes, width = states_ref.shape
    att = q_ref.shape[1]
    pairs = att // LANES
    n_var = dec_ref.shape[0]
    points = target_ref.shape[1]
    scale = 1.0 / math.sqrt(HEAD_DIM)
    has_left = s > 0
    has_right = s < n_s - 1
    sides = ((0, -1, has_left), (1, 1, has_right))
    rings = ((0, -1, ring > 0), (1, 1, ring < outer - 1))

    def remote(src, dst, send_sem, recv_sem, ens, space):
        return pltpu.make_async_remote_copy(
            src_ref=src,
            dst_ref=dst,
            send_sem=send_sem,
            recv_sem=recv_sem,
            device_id=(ens, space),
            device_id_type=pl.DeviceIdType.MESH,
        )

    def received(dst, sem):
        remote(dst, dst, sem, sem, e, s).wait_recv()

    def sent(src, sem):
        remote(src, src, sem, sem, e, s).wait_send()

    loads = {}
    for i, (name, source, held) in enumerate(
        (
            ("states", states_hbm, states_ref),
            ("dec", dec_hbm, dec_ref),
            ("edges", edges_hbm, edges_ref),
            ("ew", ew_hbm, ew_ref),
            ("k", k_hbm, k_ref),
            ("v", v_hbm, v_ref),
            ("target", target_hbm, target_ref),
            ("area", area_hbm, area_ref),
            ("var", var_hbm, var_ref),
            ("win", win_hbm, win_ref),
            ("ow", ow_hbm, ow_ref),
            ("q", q_hbm, q_ref),
        )
    ):
        loads[name] = pltpu.make_async_copy(source, held, load_sem.at[i])

    def loaded(*wanted):
        for name in wanted:
            loads[name].wait()

    for load in loads.values():
        load.start()

    barrier = pltpu.get_barrier_semaphore()

    def under(present, action):
        if present is None:
            action()
        else:
            pl.when(present)(action)

    def signal(semaphore, ens, space):
        pl.semaphore_signal(
            semaphore,
            inc=1,
            device_id=(ens, space),
            device_id_type=pl.DeviceIdType.MESH,
        )

    near = [
        (lax.rem(e + r, n_e), s + shift, present)
        for shift, present in ((-1, has_left), (1, has_right), (0, None))
        for r in range(n_e)
        if r or shift
    ] + [(e, s + shift * inner, present) for _, shift, present in rings if inner > 1]

    for ens, space, present in near:
        under(present, functools.partial(signal, barrier, ens, space))

    def hello():
        for side, shift, present in rings:
            under(
                present,
                functools.partial(signal, hello_sem.at[1 - side], e, s + shift * inner),
            )

    def hello_wait():
        for side, _, present in rings:
            under(present, functools.partial(pl.semaphore_wait, hello_sem.at[side], 1))

    for slot, _, present in sides:

        @pl.when(jnp.logical_not(present))
        def _():
            kh[slot] = jnp.zeros(kh.shape[1:], BF16)
            text[2 * slot] = jnp.zeros(text.shape[1:], BF16)
            qrecv[slot] = jnp.zeros(qrecv.shape[1:], BF16)
            brecv[slot] = jnp.zeros(brecv.shape[1:], BF16)

    decp[...] = jnp.zeros(decp.shape, BF16)
    loaded("states", "dec")
    decp[0:n_var, :] = dec_ref[...]
    text[1, e] = dot(decp[...], states_ref[...], NT).astype(BF16)
    peers = sum(1 if present is None else present.astype(jnp.int32) for _, _, present in near)
    pl.semaphore_wait(barrier, peers)

    for r in range(n_e):
        ens = lax.rem(e + r, n_e)
        for shift, present in ((-1, has_left), (1, has_right), (0, None)):
            if r or shift:
                out = remote(
                    text.at[1, e],
                    text.at[1 - shift, e],
                    t_s.at[1 + shift],
                    t_r.at[1 - shift],
                    ens,
                    s + shift,
                )
                under(present, out.start)
    if outer > 2:
        hello()

    def kv_copy(slot, shift, item):
        return remote(
            k_ref if item == 0 else v_ref,
            kh.at[1 - slot, item],
            kv_s.at[slot],
            kv_r.at[1 - slot],
            e,
            s + shift,
        )

    def start_kv():
        for slot, shift, present in sides:
            for item in range(2):
                under(present, kv_copy(slot, shift, item).start)

    loaded("k", "v")
    start_kv()

    loaded("edges", "ew")
    first = (s - 1) * nodes
    chunk = nodes
    for part in range(3):
        node_ids = first + part * chunk + lax.broadcasted_iota(jnp.int32, (chunk, points), 0)
        total = jnp.zeros((chunk, points), F32)
        for slot in range(edges_ref.shape[0]):
            total = total + jnp.where(
                node_ids == edges_ref[slot : slot + 1, :], ew_ref[slot : slot + 1, :], 0.0
            )
        wt[part * chunk : (part + 1) * chunk, :] = total.astype(BF16)

    loaded("target", "area", "var", "win", "q", "ow")
    mix[...] = dot(decp[...], ow_ref[...], NT).astype(BF16)

    if n_e > 1:
        received(text.at[1, pl.ds(0, n_e - 1)], t_r.at[1])
    for slot, _, present in sides:
        under(present, functools.partial(received, text.at[2 * slot], t_r.at[2 * slot]))
    if outer > 2:
        hello_wait()
    if outer > 3:
        hello()

    def predictions(member):
        cat = jnp.concatenate([text[i, member] for i in range(3)], axis=1)
        return dot(cat, wt[...])[0:n_var].astype(BF16).astype(F32)

    own_pred = predictions(e)
    slopes = smooth_slope(own_pred - target_ref[...])
    pair_sum = jnp.zeros_like(own_pred)
    for r in range(1, n_e):
        pair_sum = pair_sum + smooth_slope(own_pred - predictions(lax.rem(e + r, n_e)))
    slopes = slopes - pair_sum / (n_e - 1)
    square = (n_var, n_var)
    diagonal = lax.broadcasted_iota(jnp.int32, square, 0) == lax.broadcasted_iota(
        jnp.int32, square, 1
    )
    var_column = jnp.sum(jnp.where(diagonal, var_ref[...], 0.0), axis=1, keepdims=True)
    gp[...] = jnp.zeros(gp.shape, BF16)
    gp[0:n_var, :] = (area_ref[...] * var_column * slopes).astype(BF16)
    q_ext = dot(gp[...], wt[...], NT)
    qsend[0] = q_ext[:, 0:nodes].astype(BF16)
    qsend[1] = q_ext[:, 2 * nodes :].astype(BF16)

    for slot, shift, present in sides:
        out = remote(
            qsend.at[slot], qrecv.at[1 - slot], q_s.at[slot], q_r.at[1 - slot], e, s + shift
        )
        under(present, out.start)

    blocks = win_ref.shape[0]
    key_place = first + lax.broadcasted_iota(jnp.int32, (1, 3 * nodes), 1)
    inside_rows = [
        (key_place >= win_ref[b : b + 1, 0:1]) & (key_place < win_ref[b : b + 1, 1:2])
        for b in range(blocks)
    ]
    heads_per = LANES // HEAD_DIM
    lane_head = lax.broadcasted_iota(jnp.int32, (nodes, LANES), 1) // HEAD_DIM

    def split_heads(x):
        x = x.astype(F32)
        return jnp.concatenate(
            [jnp.where(lane_head == h, x, 0.0).astype(BF16) for h in range(heads_per)], axis=0
        )

    def merge_heads(x):
        out = x[0:nodes]
        for h in range(1, heads_per):
            out = jnp.where(lane_head == h, x[h * nodes : (h + 1) * nodes], out)
        return out

    def extended(item, own_ref, columns):
        return jnp.concatenate(
            [kh[0, item, :, columns], own_ref[:, columns], kh[1, item, :, columns]], axis=0
        )

    def columns_of(p):
        return slice(p * LANES, (p + 1) * LANES)

    for p in range(pairs):
        qs[p] = split_heads(q_ref[:, columns_of(p)].astype(F32) * scale)

    for slot, _, present in sides:
        under(present, functools.partial(received, qrecv.at[slot], q_r.at[slot]))
    q_own = q_ext[:, nodes : 2 * nodes] + qrecv[0].astype(F32) + qrecv[1].astype(F32)
    q_rows = q_own.T.astype(BF16)
    dec_term = dot(q_own.astype(BF16), states_ref[...])
    var_rows, lanes = dsend.shape[1:]
    for c in range(group):
        dsend[c] = dec_term[0:var_rows, c * lanes : (c + 1) * lanes].astype(BF16)

    def plane_start(which):
        @pl.loop(1, group)
        def _(i):
            to = lax.rem(mine + i, group)
            ens, row = lax.div(to, inner), lax.rem(to, inner)
            source, target, s_sem, r_sem = (
                (dsend.at[to], drecv.at[mine], d_s, d_r),
                (csend.at[row], crecv.at[mine], c_s, c_r),
                (agsend, dall.at[mine], a_s, a_r),
            )[which]
            remote(source, target, s_sem, r_sem, ens, ring * inner + row).start()

    def outer_start(which):
        @pl.loop(1, outer)
        def _(i):
            to = lax.rem(ring + i, outer)
            source, target, s_sem, r_sem = (
                (zsend, zrecv.at[ring], z_s, z_r),
                (fsend.at[to], frecv.at[ring], f_s, f_r),
            )[which]
            remote(source, target, s_sem, r_sem, e, to * inner + seat).start()

    plane_start(0)
    for slot, _, present in sides:
        under(present, functools.partial(received, kh.at[slot], kv_r.at[slot]))

    for p in range(pairs):
        columns = columns_of(p)
        scores = dot(qs[p], extended(0, k_ref, columns), NT)
        if blocks == 1:
            scores = jnp.where(inside_rows[0], scores, MASKED_SCORE)
        else:
            scores = jnp.concatenate(
                [
                    jnp.where(
                        inside_rows[i % blocks],
                        scores[i * BLOCK : (i + 1) * BLOCK],
                        MASKED_SCORE,
                    )
                    for i in range(blocks * heads_per)
                ],
                axis=0,
            )
        exponent = jnp.exp(scores - jnp.max(scores, axis=-1, keepdims=True))
        attn_prob = exponent * (1.0 / jnp.sum(exponent, axis=-1, keepdims=True))
        prob[p] = attn_prob
        ao[:, columns] = merge_heads(
            dot(attn_prob.astype(BF16), extended(1, v_ref, columns))
        ).astype(BF16)

    wo_rows = fsend.shape[1]
    wo_term = dot(ao[...], q_rows, TN)
    for c in range(inner):
        for o in range(outer):
            top = (o * inner + c) * wo_rows
            csend[c, o * wo_rows : (o + 1) * wo_rows] = wo_term[top : top + wo_rows].astype(BF16)
    plane_start(1)
    drecv[mine] = dsend[mine]
    crecv[mine] = csend[seat]
    go[...] = dot(q_rows, mix[...]).astype(BF16)

    for p in range(pairs):
        columns = columns_of(p)
        grads = split_heads(go[:, columns])
        attn_prob = prob[p]
        grad_prob = dot(grads, extended(1, v_ref, columns), NT)
        row_delta = jnp.sum(attn_prob * grad_prob, axis=-1, keepdims=True)
        grad_scores = (attn_prob * (grad_prob - row_delta)).astype(BF16)
        value_term = dot(attn_prob.astype(BF16), grads, TN)
        key_term = dot(grad_scores, qs[p], TN)
        for item, term, mid in ((0, key_term, kmid), (1, value_term, vmid)):
            bsend[0, p, item] = term[0:nodes].astype(BF16)
            bsend[1, p, item] = term[2 * nodes :].astype(BF16)
            mid[:, columns] = term[nodes : 2 * nodes]
        for slot, shift, present in sides:
            out = remote(
                bsend.at[slot, p],
                brecv.at[1 - slot, p],
                b_s.at[slot],
                b_r.at[1 - slot],
                e,
                s + shift,
            )
            under(present, out.start)
        gq_ref[:, columns] = (
            merge_heads(dot(grad_scores, extended(0, k_ref, columns))) * scale
        ).astype(BF16)

    gs_ref[...] = dot(q_rows, decp[...]).astype(BF16)
    received(drecv.at[pl.ds(0, group - 1)], d_r)
    dec_plane = jnp.sum(drecv[...].astype(F32), axis=0).astype(BF16)
    zsend[...] = dec_plane
    zrecv[ring] = dec_plane
    if outer > 3:
        hello_wait()
    for _ in range(outer - 4):
        hello()
        hello_wait()
    outer_start(0)

    received(crecv.at[pl.ds(0, group - 1)], c_r)
    wo_plane = jnp.sum(crecv[...].astype(F32), axis=0).astype(BF16)
    for o in range(outer):
        fsend[o] = wo_plane[o * wo_rows : (o + 1) * wo_rows]
    frecv[ring] = fsend[ring]
    outer_start(1)

    if outer > 1:
        received(zrecv.at[pl.ds(0, outer - 1)], z_r)
    dec_sum = jnp.sum(zrecv[...].astype(F32), axis=0).astype(BF16)
    agsend[...] = dec_sum
    dall[mine] = dec_sum
    plane_start(2)

    for slot, _, present in sides:
        under(present, functools.partial(received, brecv.at[slot], b_r.at[slot]))
    for p in range(pairs):
        columns = columns_of(p)
        for item, mid, out_ref in ((0, kmid, gk_ref), (1, vmid, gv_ref)):
            out_ref[:, columns] = (
                mid[:, columns]
                + brecv[0, p, item].astype(F32)
                + brecv[1, p, item].astype(F32)
            ).astype(BF16)

    if outer > 1:
        received(frecv.at[pl.ds(0, outer - 1)], f_r)
    wo_sum = jnp.sum(frecv[...].astype(F32), axis=0)
    gwo_ref[...] = dot(wo_sum.astype(BF16), decp[...])

    for slot, shift, present in sides:

        def drain():
            for _ in range(n_e):
                sent(text.at[1, 0], t_s.at[1 + shift])
            sent(kh.at[slot], kv_s.at[slot])
            sent(qsend.at[slot], q_s.at[slot])
            sent(bsend.at[slot], b_s.at[slot])

        under(present, drain)
    if n_e > 1:
        sent(text.at[1, pl.ds(0, n_e - 1)], t_s.at[1])
    sent(dsend.at[pl.ds(0, group - 1)], d_s)
    sent(crecv.at[pl.ds(0, group - 1)], c_s)
    if outer > 1:
        sent(zrecv.at[pl.ds(0, outer - 1)], z_s)
        sent(frecv.at[pl.ds(0, outer - 1)], f_s)
    received(dall.at[pl.ds(0, group - 1)], a_r)
    for c in range(group):
        gdec_ref[:, c * lanes : (c + 1) * lanes] = dall[c].astype(F32)[0:n_var]
    sent(dall.at[pl.ds(0, group - 1)], a_s)


def hand_over(*refs):
    count = (len(refs) - 1) // 2
    sems = refs[-1]
    copies = [
        pltpu.make_async_copy(refs[i], refs[count + i], sems.at[i]) for i in range(count)
    ]
    for copy in copies:
        copy.start()
    for copy in copies:
        copy.wait()


def per_device(
    node_states,
    query,
    key,
    value,
    out_weight,
    dec_weight,
    target,
    area_weight,
    var_weight,
    edges,
    edge_weight,
    windows,
):
    n_e, n_s = lax.axis_size("ens"), lax.axis_size("space")
    inner = math.gcd(n_s, INNER)
    outer, group = n_s // inner, n_e * inner
    nodes, width = node_states.shape[1:]
    att = query.shape[2]
    n_var, points = target.shape
    pairs = att // LANES
    var_pad = -(-n_var // LANES) * LANES
    var_rows = -(-n_var // 16) * 16
    lanes = width // group
    wo_rows = att // n_s
    span = 3 * nodes
    heads_per = LANES // HEAD_DIM
    dma = pltpu.SemaphoreType.DMA
    operands = (
        node_states[0],
        query[0],
        key[0],
        value[0],
        out_weight,
        dec_weight,
        target,
        area_weight[None, :],
        var_weight[None, :],
        edges,
        edge_weight,
        windows.T,
    )
    outs = pl.pallas_call(
        functools.partial(kernel, n_e, n_s),
        out_shape=(
            pltpu.VMEM((nodes, width), BF16),
            pltpu.VMEM((nodes, att), BF16),
            pltpu.VMEM((nodes, att), BF16),
            pltpu.VMEM((nodes, att), BF16),
            pltpu.VMEM((wo_rows, width), F32),
            pltpu.VMEM((n_var, width), F32),
        ),
        in_specs=[pl.BlockSpec(memory_space=pltpu.HBM)] * len(operands),
        out_specs=[pl.BlockSpec(memory_space=pltpu.VMEM)] * 6,
        scratch_shapes=[pltpu.VMEM(x.shape, x.dtype) for x in operands]
        + [
            pltpu.VMEM((var_pad, width), BF16),
            pltpu.VMEM((var_pad, att), BF16),
            pltpu.VMEM((span, points), BF16),
            pltpu.VMEM((2, 2, nodes, att), BF16),
            pltpu.VMEM((3, n_e, var_pad, nodes), BF16),
            pltpu.VMEM((var_pad, points), BF16),
            pltpu.VMEM((2, var_pad, nodes), BF16),
            pltpu.VMEM((2, var_pad, nodes), BF16),
            pltpu.VMEM((pairs, heads_per * nodes, LANES), BF16),
            pltpu.VMEM((pairs, heads_per * nodes, span), F32),
            pltpu.VMEM((nodes, att), BF16),
            pltpu.VMEM((nodes, att), BF16),
            pltpu.VMEM((nodes, att), F32),
            pltpu.VMEM((nodes, att), F32),
            pltpu.VMEM((2, pairs, 2, nodes, LANES), BF16),
            pltpu.VMEM((2, pairs, 2, nodes, LANES), BF16),
            pltpu.VMEM((inner, outer * wo_rows, var_pad), BF16),
            pltpu.VMEM((group, outer * wo_rows, var_pad), BF16),
            pltpu.VMEM((group, var_rows, lanes), BF16),
            pltpu.VMEM((group, var_rows, lanes), BF16),
            pltpu.VMEM((var_rows, lanes), BF16),
            pltpu.VMEM((outer, var_rows, lanes), BF16),
            pltpu.VMEM((outer, wo_rows, var_pad), BF16),
            pltpu.VMEM((outer, wo_rows, var_pad), BF16),
            pltpu.VMEM((var_rows, lanes), BF16),
            pltpu.VMEM((group, var_rows, lanes), BF16),
            dma((2,)),
            dma((2,)),
            dma((3,)),
            dma((3,)),
            dma((2,)),
            dma((2,)),
            dma((2,)),
            dma((2,)),
            dma,
            dma,
            dma,
            dma,
            dma,
            dma,
            dma,
            dma,
            dma,
            dma,
            dma((len(operands),)),
            pltpu.SemaphoreType.REGULAR((2,)),
        ],
        compiler_params=pltpu.CompilerParams(
            collective_id=0, has_side_effects=True, vmem_limit_bytes=40_000_000
        ),
    )(*(pltpu.with_memory_space_constraint(x, pltpu.HBM) for x in operands))
    outs = pl.pallas_call(
        hand_over,
        out_shape=[jax.ShapeDtypeStruct(x.shape, x.dtype) for x in outs],
        in_specs=[pl.BlockSpec(memory_space=pltpu.VMEM)] * len(outs),
        out_specs=[pl.BlockSpec(memory_space=pltpu.HBM)] * len(outs),
        scratch_shapes=[dma((len(outs),))],
        compiler_params=pltpu.CompilerParams(vmem_limit_bytes=20_000_000),
    )(*outs)
    grad_states, grad_query, grad_key, grad_value, grad_wo, grad_dec = outs
    return (
        grad_states[None],
        grad_query[None],
        grad_key[None],
        grad_value[None],
        grad_wo,
        grad_dec,
    )


def solution(mesh):
    banded = P("ens", "space", None)
    in_specs = (
        banded,
        banded,
        banded,
        banded,
        P(),
        P(),
        P(None, "space"),
        P("space"),
        P(),
        P(None, "space"),
        P(None, "space"),
        P(None, "space"),
    )
    out_specs = (banded, banded, banded, banded, P("space", None), P())
    return jax.shard_map(
        per_device, mesh=mesh, in_specs=in_specs, out_specs=out_specs, check_vma=False
    )
```

```python
import functools
import math

import jax
import jax.numpy as jnp
from jax import lax
from jax.experimental import pallas as pl
from jax.experimental.pallas import tpu as pltpu
from jax.sharding import PartitionSpec as P

HEAD_DIM = 64
BLOCK = 128
INNER = 4
LANES = 128
SMOOTH_SQUARE = 0.0625
MASKED_SCORE = -1e30
F32 = jnp.float32
BF16 = jnp.bfloat16
NT = (((1,), (1,)), ((), ()))
TN = (((0,), (0,)), ((), ()))


def smooth_slope(diff_value):
    return diff_value * lax.rsqrt(diff_value * diff_value + SMOOTH_SQUARE)


def dot(a, b, dims=(((1,), (0,)), ((), ()))):
    return lax.dot_general(a, b, dims, preferred_element_type=F32)


def kernel(
    n_e,
    n_s,
    states_hbm,
    q_hbm,
    k_hbm,
    v_hbm,
    ow_hbm,
    dec_hbm,
    target_hbm,
    area_hbm,
    var_hbm,
    edges_hbm,
    ew_hbm,
    win_hbm,
    gs_ref,
    gq_ref,
    gk_ref,
    gv_ref,
    gwo_ref,
    gdec_ref,
    states_ref,
    q_ref,
    k_ref,
    v_ref,
    ow_ref,
    dec_ref,
    target_ref,
    area_ref,
    var_ref,
    edges_ref,
    ew_ref,
    win_ref,
    decp,
    mix,
    wt,
    kh,
    text,
    gp,
    qsend,
    qrecv,
    qs,
    prob,
    ao,
    go,
    kmid,
    vmid,
    gsc,
    qn,
    rows_own,
    rows_near,
    slab,
    stat,
    stat_near,
    go_near,
    csend,
    cpair,
    cmid,
    crecv,
    dsend,
    dpair,
    dmid,
    drecv,
    zsend,
    zrecv,
    fsend,
    frecv,
    agsend,
    dall,
    kv_s,
    kv_r,
    t_s,
    t_r,
    q_s,
    q_r,
    qn_s,
    qn_r,
    n_s_sem,
    n_r_sem,
    st_s,
    st_r,
    c_s,
    c_r,
    d_s,
    d_r,
    a_s,
    a_r,
    z_s,
    z_r,
    f_s,
    f_r,
    pd_s,
    pd_r,
    pc_s,
    pc_r,
    pa_s,
    pa_r,
    load_sem,
    hello_sem,
):
    e = lax.axis_index("ens")
    s = lax.axis_index("space")
    inner = math.gcd(n_s, INNER)
    outer = n_s // inner
    group = n_e * inner
    ring, seat = lax.div(s, inner), lax.rem(s, inner)
    pair = math.gcd(inner, 2)
    rows_in = inner // pair
    half = group // pair
    place, parity = lax.div(seat, pair), lax.rem(seat, pair)
    mine = e * rows_in + place
    spots = n_e * outer
    everyone = half * outer
    flat = drecv.shape[0] == everyone
    seat_all = mine * outer + ring
    nodes, width = states_ref.shape
    att = q_ref.shape[1]
    pairs = att // LANES
    n_var = dec_ref.shape[0]
    points = target_ref.shape[1]
    scale = 1.0 / math.sqrt(HEAD_DIM)
    has_left = s > 0
    has_right = s < n_s - 1
    sides = ((0, -1, has_left), (1, 1, has_right))
    rings = ((0, -1, ring > 0), (1, 1, ring < outer - 1))

    def remote(src, dst, send_sem, recv_sem, ens, space):
        return pltpu.make_async_remote_copy(
            src_ref=src,
            dst_ref=dst,
            send_sem=send_sem,
            recv_sem=recv_sem,
            device_id=(ens, space),
            device_id_type=pl.DeviceIdType.MESH,
        )

    def received(dst, sem):
        remote(dst, dst, sem, sem, e, s).wait_recv()

    def sent(src, sem):
        remote(src, src, sem, sem, e, s).wait_send()

    loads = {}
    for i, (name, source, held) in enumerate(
        (
            ("states", states_hbm, states_ref),
            ("dec", dec_hbm, dec_ref),
            ("edges", edges_hbm, edges_ref),
            ("ew", ew_hbm, ew_ref),
            ("k", k_hbm, k_ref),
            ("v", v_hbm, v_ref),
            ("target", target_hbm, target_ref),
            ("area", area_hbm, area_ref),
            ("var", var_hbm, var_ref),
            ("win", win_hbm, win_ref),
            ("ow", ow_hbm, ow_ref),
            ("q", q_hbm, q_ref),
        )
    ):
        loads[name] = pltpu.make_async_copy(source, held, load_sem.at[i])

    def loaded(*wanted):
        for name in wanted:
            loads[name].wait()

    for load in loads.values():
        load.start()

    barrier = pltpu.get_barrier_semaphore()

    def under(present, action):
        if present is None:
            action()
        else:
            pl.when(present)(action)

    def signal(semaphore, ens, space):
        pl.semaphore_signal(
            semaphore,
            inc=1,
            device_id=(ens, space),
            device_id_type=pl.DeviceIdType.MESH,
        )

    near = [
        (lax.rem(e + r, n_e), s + shift, present)
        for shift, present in ((-1, has_left), (1, has_right), (0, None))
        for r in range(n_e)
        if r or shift
    ] + [(e, s + shift * inner, present) for _, shift, present in rings if inner > 1]

    for ens, space, present in near:
        under(present, functools.partial(signal, barrier, ens, space))

    def hello():
        for side, shift, present in rings:
            under(
                present,
                functools.partial(signal, hello_sem.at[1 - side], e, s + shift * inner),
            )

    def hello_wait():
        for side, _, present in rings:
            under(present, functools.partial(pl.semaphore_wait, hello_sem.at[side], 1))

    for slot, _, present in sides:

        @pl.when(jnp.logical_not(present))
        def _():
            kh[slot] = jnp.zeros(kh.shape[1:], BF16)
            text[2 * slot] = jnp.zeros(text.shape[1:], BF16)
            qrecv[slot] = jnp.zeros(qrecv.shape[1:], BF16)
            qn[slot] = jnp.zeros(qn.shape[1:], BF16)
            rows_near[slot] = jnp.zeros(rows_near.shape[1:], BF16)
            stat_near[slot] = jnp.zeros(stat_near.shape[1:], F32)

    decp[...] = jnp.zeros(decp.shape, BF16)
    loaded("states", "dec")
    decp[0:n_var, :] = dec_ref[...]
    text[1, e] = dot(decp[...], states_ref[...], NT).astype(BF16)
    peers = sum(1 if present is None else present.astype(jnp.int32) for _, _, present in near)
    pl.semaphore_wait(barrier, peers)

    for r in range(n_e):
        ens = lax.rem(e + r, n_e)
        for shift, present in ((-1, has_left), (1, has_right), (0, None)):
            if r or shift:
                out = remote(
                    text.at[1, e],
                    text.at[1 - shift, e],
                    t_s.at[1 + shift],
                    t_r.at[1 - shift],
                    ens,
                    s + shift,
                )
                under(present, out.start)
    if outer > 1:
        hello()

    def kv_copy(slot, shift, item):
        return remote(
            k_ref if item == 0 else v_ref,
            kh.at[1 - slot, item],
            kv_s.at[slot, item],
            kv_r.at[1 - slot, item],
            e,
            s + shift,
        )

    def to_sides(src, dst, s_sem, r_sem):
        for slot, shift, present in sides:
            out = remote(
                src, dst.at[1 - slot], s_sem.at[slot], r_sem.at[1 - slot], e, s + shift
            )
            under(present, out.start)

    def start_kv(item):
        for slot, shift, present in sides:
            under(present, kv_copy(slot, shift, item).start)

    loaded("k", "v")
    start_kv(0)

    loaded("edges", "ew")
    first = (s - 1) * nodes
    chunk = nodes
    for part in range(3):
        node_ids = first + part * chunk + lax.broadcasted_iota(jnp.int32, (chunk, points), 0)
        total = jnp.zeros((chunk, points), F32)
        for slot in range(edges_ref.shape[0]):
            total = total + jnp.where(
                node_ids == edges_ref[slot : slot + 1, :], ew_ref[slot : slot + 1, :], 0.0
            )
        wt[part * chunk : (part + 1) * chunk, :] = total.astype(BF16)

    loaded("target", "area", "var", "win", "q", "ow")
    mix[...] = dot(decp[...], ow_ref[...], NT).astype(BF16)

    if n_e > 1:
        received(text.at[1, pl.ds(0, n_e - 1)], t_r.at[1])
    for slot, _, present in sides:
        under(present, functools.partial(received, text.at[2 * slot], t_r.at[2 * slot]))
    if outer > 1:
        hello_wait()
        hello()

    def predictions(member):
        cat = jnp.concatenate([text[i, member] for i in range(3)], axis=1)
        return dot(cat, wt[...])[0:n_var].astype(BF16).astype(F32)

    own_pred = predictions(e)
    slopes = smooth_slope(own_pred - target_ref[...])
    pair_sum = jnp.zeros_like(own_pred)
    for r in range(1, n_e):
        pair_sum = pair_sum + smooth_slope(own_pred - predictions(lax.rem(e + r, n_e)))
    slopes = slopes - pair_sum / (n_e - 1)
    square = (n_var, n_var)
    diagonal = lax.broadcasted_iota(jnp.int32, square, 0) == lax.broadcasted_iota(
        jnp.int32, square, 1
    )
    var_column = jnp.sum(jnp.where(diagonal, var_ref[...], 0.0), axis=1, keepdims=True)
    gp[...] = jnp.zeros(gp.shape, BF16)
    gp[0:n_var, :] = (area_ref[...] * var_column * slopes).astype(BF16)
    q_ext = dot(gp[...], wt[...], NT)
    qsend[0] = q_ext[:, 0:nodes].astype(BF16)
    qsend[1] = q_ext[:, 2 * nodes :].astype(BF16)

    for slot, shift, present in sides:
        out = remote(
            qsend.at[slot], qrecv.at[1 - slot], q_s.at[slot], q_r.at[1 - slot], e, s + shift
        )
        under(present, out.start)
    start_kv(1)

    blocks = win_ref.shape[0]
    key_place = first + lax.broadcasted_iota(jnp.int32, (1, 3 * nodes), 1)
    inside_rows = [
        (key_place >= win_ref[b : b + 1, 0:1]) & (key_place < win_ref[b : b + 1, 1:2])
        for b in range(blocks)
    ]
    heads_per = LANES // HEAD_DIM
    lane_head = lax.broadcasted_iota(jnp.int32, (nodes, LANES), 1) // HEAD_DIM

    def split_heads(x):
        x = x.astype(F32)
        return jnp.concatenate(
            [jnp.where(lane_head == h, x, 0.0).astype(BF16) for h in range(heads_per)], axis=0
        )

    def merge_heads(x):
        out = x[0:nodes]
        for h in range(1, heads_per):
            out = jnp.where(lane_head == h, x[h * nodes : (h + 1) * nodes], out)
        return out

    def extended(item, own_ref, columns):
        return jnp.concatenate(
            [kh[0, item, :, columns], own_ref[:, columns], kh[1, item, :, columns]], axis=0
        )

    def columns_of(p):
        return slice(p * LANES, (p + 1) * LANES)

    for p in range(pairs):
        qs[p] = split_heads(q_ref[:, columns_of(p)].astype(F32) * scale)

    def arrived(item):
        for slot, _, present in sides:
            under(present, functools.partial(received, kh.at[slot, item], kv_r.at[slot, item]))

    arrived(0)
    if outer > 2:
        hello_wait()
        hello()
    heads_rows = heads_per * nodes
    stat_lane = lax.broadcasted_iota(jnp.int32, (heads_rows, LANES), 1)

    def put_stat(held, at, column):
        return jnp.where(stat_lane == at, column, held)

    stats = jnp.zeros((heads_rows, LANES), F32)
    for bound in range(2):
        edge = jnp.concatenate(
            [
                jnp.broadcast_to(
                    win_ref[i % blocks : i % blocks + 1, bound : bound + 1].astype(F32),
                    (BLOCK, 1),
                )
                for i in range(blocks * heads_per)
            ],
            axis=0,
        )
        stats = put_stat(stats, 3 * pairs + bound, edge)
    for p in range(pairs):
        columns = columns_of(p)
        scores = dot(qs[p], extended(0, k_ref, columns), NT)
        if blocks == 1:
            scores = jnp.where(inside_rows[0], scores, MASKED_SCORE)
        else:
            scores = jnp.concatenate(
                [
                    jnp.where(
                        inside_rows[i % blocks],
                        scores[i * BLOCK : (i + 1) * BLOCK],
                        MASKED_SCORE,
                    )
                    for i in range(blocks * heads_per)
                ],
                axis=0,
            )
        row_max = jnp.max(scores, axis=-1, keepdims=True)
        exponent = jnp.exp(scores - row_max)
        inverse = 1.0 / jnp.sum(exponent, axis=-1, keepdims=True)
        prob[p] = exponent * inverse
        stats = put_stat(stats, p, row_max)
        stats = put_stat(stats, pairs + p, inverse)

    slab[...] = stats
    if outer > 3:
        hello_wait()
        hello()
    for slot, _, present in sides:
        under(present, functools.partial(received, qrecv.at[slot], q_r.at[slot]))
    q_own = q_ext[:, nodes : 2 * nodes] + qrecv[0].astype(F32) + qrecv[1].astype(F32)
    q_rows = q_own.T.astype(BF16)
    rows_own[...] = q_rows
    dec_term = dot(q_own.astype(BF16), states_ref[...])
    var_rows, lanes = dsend.shape[2:]
    for c in range(group):
        dsend[c // half, c % half] = dec_term[0:var_rows, c * lanes : (c + 1) * lanes].astype(BF16)

    def pair_start(source, target, s_sem, r_sem):
        if pair > 1:
            remote(source, target, s_sem, r_sem, e, s + 1 - 2 * parity).start()

    def plane_start(source, target, s_sem, r_sem):
        @pl.loop(1, half)
        def _(i):
            to = lax.rem(mine + i, half)
            ens, row = lax.div(to, rows_in), lax.rem(to, rows_in)
            remote(
                source if source is agsend else source.at[to],
                target,
                s_sem,
                r_sem,
                ens,
                ring * inner + row * pair + parity,
            ).start()

    pair_start(dsend.at[1 - parity], dpair, pd_s, pd_r)
    to_sides(rows_own, rows_near, n_s_sem, n_r_sem)
    go[...] = dot(q_rows, mix[...]).astype(BF16)
    if pair > 1:
        received(dpair, pd_r)
        dmid[...] = (dsend[parity].astype(F32) + dpair[...].astype(F32)).astype(BF16)
    else:
        dmid[...] = dsend[parity]
    if outer > 1:
        hello_wait()
    for _ in range(outer - 4):
        hello()
        hello_wait()
    if flat:
        piece = drecv.shape[1]

        def all_start(source_of, target, s_sem, r_sem):
            for far in range(outer):
                around = lax.rem(ring + far, outer)
                for across in range(n_e):
                    ens = lax.rem(e + across, n_e)
                    for along in range(rows_in):
                        if far or across or along:
                            row = lax.rem(place + along, rows_in)
                            remote(
                                source_of(ens * rows_in + row, row, around),
                                target,
                                s_sem,
                                r_sem,
                                ens,
                                around * inner + row * pair + parity,
                            ).start()

        def piece_rows(around):
            return pl.ds(pl.multiple_of(around * piece, piece), piece)

        all_start(
            lambda member, row, around: dmid.at[member, piece_rows(around)],
            drecv.at[seat_all],
            d_s,
            d_r,
        )
        drecv[seat_all] = dmid[mine, piece_rows(ring)]
    else:
        plane_start(dmid, drecv.at[mine], d_s, d_r)
        drecv[mine] = dmid[mine]
    arrived(1)
    for p in range(pairs):
        columns = columns_of(p)
        ao[:, columns] = merge_heads(
            dot(prob[p].astype(BF16), extended(1, v_ref, columns))
        ).astype(BF16)
    wo_rows = fsend.shape[1]
    wo_term = dot(ao[...], q_rows, TN)
    for c in range(inner):
        for o in range(outer):
            top = (o * inner + c) * wo_rows
            csend[c % pair, c // pair, o * wo_rows : (o + 1) * wo_rows] = wo_term[
                top : top + wo_rows
            ].astype(BF16)
    pair_start(csend.at[1 - parity], cpair, pc_s, pc_r)
    def wo_across():
        if pair > 1:
            received(cpair, pc_r)
            cmid[...] = (csend[parity].astype(F32) + cpair[...].astype(F32)).astype(BF16)
        else:
            cmid[...] = csend[parity]

        if flat:

            def wo_part(around):
                return pl.ds(pl.multiple_of(around * wo_rows, wo_rows), wo_rows)

            all_start(
                lambda member, row, around: cmid.at[row, wo_part(around)],
                frecv.at[seat_all],
                f_s,
                f_r,
            )
            frecv[seat_all] = cmid[place, wo_part(ring)]
            return

        @pl.loop(1, rows_in)
        def _(i):
            to = lax.rem(place + i, rows_in)
            remote(
                cmid.at[to], crecv.at[place], c_s, c_r, e, ring * inner + to * pair + parity
            ).start()

        crecv[place] = cmid[place]

    def gather_flat():
        received(drecv.at[pl.ds(0, everyone - 1)], d_r)
        dec_sum = jnp.sum(drecv[...].astype(F32), axis=0).astype(BF16)
        agsend[...] = dec_sum
        dall[parity, mine, piece_rows(ring)] = dec_sum
        all_start(
            lambda member, row, around: agsend,
            dall.at[parity, mine, piece_rows(ring)],
            a_s,
            a_r,
        )

    def gather_planes():
        received(drecv.at[pl.ds(0, half - 1)], d_r)
        dec_plane = jnp.sum(drecv[...].astype(F32), axis=0).astype(BF16)
        zsend[...] = dec_plane
        zrecv[ring] = dec_plane

        @pl.loop(1, outer)
        def _(i):
            to = lax.rem(ring + i, outer)
            remote(zsend, zrecv.at[ring], z_s, z_r, e, to * inner + seat).start()

        if rows_in > 1:
            received(crecv.at[pl.ds(0, rows_in - 1)], c_r)
        wo_plane = jnp.sum(crecv[...].astype(F32), axis=0).astype(BF16)
        for o in range(outer):
            fsend[o] = wo_plane[o * wo_rows : (o + 1) * wo_rows]
        spot = e * outer + ring
        frecv[spot] = fsend[ring]

        @pl.loop(1, spots)
        def _(i):
            to = lax.rem(spot + i, spots)
            ens, around = lax.div(to, outer), lax.rem(to, outer)
            remote(fsend.at[around], frecv.at[spot], f_s, f_r, ens, around * inner + seat).start()

        if outer > 1:
            received(zrecv.at[pl.ds(0, outer - 1)], z_r)
        dec_sum = jnp.sum(zrecv[...].astype(F32), axis=0).astype(BF16)
        agsend[...] = dec_sum
        dall[parity, mine] = dec_sum
        plane_start(agsend, dall.at[parity, mine], a_s, a_r)

    stats = slab[...]
    for p in range(pairs):
        columns = columns_of(p)
        attn_prob = prob[p]
        grad_prob = dot(split_heads(go[:, columns]), extended(1, v_ref, columns), NT)
        row_delta = jnp.sum(attn_prob * grad_prob, axis=-1, keepdims=True)
        gsc[p] = (attn_prob * (grad_prob - row_delta)).astype(BF16)
        stats = put_stat(stats, 2 * pairs + p, row_delta)
    stat[...] = stats.T[0 : stat.shape[0]]
    wo_across()
    to_sides(stat, stat_near, st_s, st_r)
    to_sides(q_ref, qn, qn_s, qn_r)
    if flat:
        gather_flat()
    for p in range(pairs):
        columns = columns_of(p)
        middle = slice(nodes, 2 * nodes)
        grads = split_heads(go[:, columns])
        kmid[:, columns] = dot(gsc[p, :, middle], qs[p], TN)
        vmid[:, columns] = dot(prob[p, :, middle].astype(BF16), grads, TN)
        gq_ref[:, columns] = (
            merge_heads(dot(gsc[p], extended(0, k_ref, columns))) * scale
        ).astype(BF16)

    gs_ref[...] = dot(q_rows, decp[...]).astype(BF16)
    if not flat:
        gather_planes()
    for slot, _, present in sides:
        under(present, functools.partial(received, rows_near.at[slot], n_r_sem.at[slot]))
        under(present, functools.partial(received, qn.at[slot], qn_r.at[slot]))
        under(present, functools.partial(received, stat_near.at[slot], st_r.at[slot]))
    for slot in range(2):
        go_near[slot] = dot(rows_near[slot], mix[...]).astype(BF16)
    key_column = (
        s * nodes + lax.broadcasted_iota(jnp.int32, (nodes, 2 * heads_rows), 0)
    ).astype(F32)

    def near_stat(at):
        return jnp.concatenate([stat_near[i, at : at + 1, :] for i in range(2)], axis=1)

    allowed = (key_column >= near_stat(3 * pairs)) & (key_column < near_stat(3 * pairs + 1))
    for p in range(pairs):
        columns = columns_of(p)
        q_near = jnp.concatenate(
            [split_heads(qn[i, :, columns].astype(F32) * scale) for i in range(2)], axis=0
        )
        g_near = jnp.concatenate([split_heads(go_near[i, :, columns]) for i in range(2)], axis=0)
        scores = dot(k_ref[:, columns], q_near, NT)
        near_prob = jnp.exp(
            jnp.where(allowed, scores - near_stat(p), MASKED_SCORE)
        ) * near_stat(pairs + p)
        near_grad = dot(v_ref[:, columns], g_near, NT)
        near_scores = near_prob * (near_grad - near_stat(2 * pairs + p))
        gv_ref[:, columns] = (
            vmid[:, columns] + dot(near_prob.astype(BF16), g_near)
        ).astype(BF16)
        gk_ref[:, columns] = (
            kmid[:, columns] + dot(near_scores.astype(BF16), q_near)
        ).astype(BF16)

    if frecv.shape[0] > 1:
        received(frecv.at[pl.ds(0, frecv.shape[0] - 1)], f_r)
    wo_sum = jnp.sum(frecv[...].astype(F32), axis=0)
    gwo_ref[...] = dot(wo_sum.astype(BF16), decp[...])

    for slot, shift, present in sides:

        def drain():
            for _ in range(n_e):
                sent(text.at[1, 0], t_s.at[1 + shift])
            for item in range(2):
                sent(kh.at[slot, item], kv_s.at[slot, item])
            sent(qsend.at[slot], q_s.at[slot])
            sent(qn.at[slot], qn_s.at[slot])
            sent(rows_own, n_s_sem.at[slot])
            sent(stat, st_s.at[slot])

        under(present, drain)
    if n_e > 1:
        sent(text.at[1, pl.ds(0, n_e - 1)], t_s.at[1])
    if pair > 1:
        sent(dpair, pd_s)
        sent(cpair, pc_s)
    parts = drecv.shape[0]
    sent(drecv.at[pl.ds(0, parts - 1)], d_s)
    if not flat:
        if rows_in > 1:
            sent(crecv.at[pl.ds(0, rows_in - 1)], c_s)
        if outer > 1:
            sent(zrecv.at[pl.ds(0, outer - 1)], z_s)
    if frecv.shape[0] > 1:
        sent(frecv.at[pl.ds(0, frecv.shape[0] - 1)], f_s)
    received(drecv.at[pl.ds(0, parts - 1)], a_r)
    pair_start(dall.at[parity], dall.at[parity], pa_s, pa_r)
    sent(drecv.at[pl.ds(0, parts - 1)], a_s)
    if pair > 1:
        received(dpair, pa_r)
    for c in range(group):
        gdec_ref[:, c * lanes : (c + 1) * lanes] = dall[c // half, c % half].astype(F32)[0:n_var]
    if pair > 1:
        sent(dpair, pa_s)


def hand_over(*refs):
    count = (len(refs) - 1) // 2
    sems = refs[-1]
    copies = [
        pltpu.make_async_copy(refs[i], refs[count + i], sems.at[i]) for i in range(count)
    ]
    for copy in copies:
        copy.start()
    for copy in copies:
        copy.wait()


def per_device(
    node_states,
    query,
    key,
    value,
    out_weight,
    dec_weight,
    target,
    area_weight,
    var_weight,
    edges,
    edge_weight,
    windows,
):
    n_e, n_s = lax.axis_size("ens"), lax.axis_size("space")
    inner = math.gcd(n_s, INNER)
    outer, group = n_s // inner, n_e * inner
    pair = math.gcd(inner, 2)
    half = group // pair
    nodes, width = node_states.shape[1:]
    att = query.shape[2]
    n_var, points = target.shape
    pairs = att // LANES
    var_pad = -(-n_var // LANES) * LANES
    flat = var_pad % (16 * outer) == 0
    var_rows = var_pad if flat else -(-n_var // 16) * 16
    piece = var_rows // outer if flat else var_rows
    lanes = width // group
    wo_rows = att // n_s
    span = 3 * nodes
    heads_per = LANES // HEAD_DIM
    stat_rows = -(-(3 * pairs + 2) // 8) * 8
    dma = pltpu.SemaphoreType.DMA
    operands = (
        node_states[0],
        query[0],
        key[0],
        value[0],
        out_weight,
        dec_weight,
        target,
        area_weight[None, :],
        var_weight[None, :],
        edges,
        edge_weight,
        windows.T,
    )
    outs = pl.pallas_call(
        functools.partial(kernel, n_e, n_s),
        out_shape=(
            pltpu.VMEM((nodes, width), BF16),
            pltpu.VMEM((nodes, att), BF16),
            pltpu.VMEM((nodes, att), BF16),
            pltpu.VMEM((nodes, att), BF16),
            pltpu.VMEM((wo_rows, width), F32),
            pltpu.VMEM((n_var, width), F32),
        ),
        in_specs=[pl.BlockSpec(memory_space=pltpu.HBM)] * len(operands),
        out_specs=[pl.BlockSpec(memory_space=pltpu.VMEM)] * 6,
        scratch_shapes=[pltpu.VMEM(x.shape, x.dtype) for x in operands]
        + [
            pltpu.VMEM((var_pad, width), BF16),
            pltpu.VMEM((var_pad, att), BF16),
            pltpu.VMEM((span, points), BF16),
            pltpu.VMEM((2, 2, nodes, att), BF16),
            pltpu.VMEM((3, n_e, var_pad, nodes), BF16),
            pltpu.VMEM((var_pad, points), BF16),
            pltpu.VMEM((2, var_pad, nodes), BF16),
            pltpu.VMEM((2, var_pad, nodes), BF16),
            pltpu.VMEM((pairs, heads_per * nodes, LANES), BF16),
            pltpu.VMEM((pairs, heads_per * nodes, span), F32),
            pltpu.VMEM((nodes, att), BF16),
            pltpu.VMEM((nodes, att), BF16),
            pltpu.VMEM((nodes, att), F32),
            pltpu.VMEM((nodes, att), F32),
            pltpu.VMEM((pairs, heads_per * nodes, span), BF16),
            pltpu.VMEM((2, nodes, att), BF16),
            pltpu.VMEM((nodes, var_pad), BF16),
            pltpu.VMEM((2, nodes, var_pad), BF16),
            pltpu.VMEM((heads_per * nodes, LANES), F32),
            pltpu.VMEM((stat_rows, heads_per * nodes), F32),
            pltpu.VMEM((2, stat_rows, heads_per * nodes), F32),
            pltpu.VMEM((2, nodes, att), BF16),
            pltpu.VMEM((pair, inner // pair, outer * wo_rows, var_pad), BF16),
            pltpu.VMEM((inner // pair, outer * wo_rows, var_pad), BF16),
            pltpu.VMEM((inner // pair, outer * wo_rows, var_pad), BF16),
            pltpu.VMEM((inner // pair, outer * wo_rows, var_pad), BF16),
            pltpu.VMEM((pair, half, var_rows, lanes), BF16),
            pltpu.VMEM((half, var_rows, lanes), BF16),
            pltpu.VMEM((half, var_rows, lanes), BF16),
            pltpu.VMEM((half * outer if flat else half, piece, lanes), BF16),
            pltpu.VMEM((var_rows, lanes), BF16),
            pltpu.VMEM((outer, var_rows, lanes), BF16),
            pltpu.VMEM((outer, wo_rows, var_pad), BF16),
            pltpu.VMEM(((half if flat else n_e) * outer, wo_rows, var_pad), BF16),
            pltpu.VMEM((piece, lanes), BF16),
            pltpu.VMEM((pair, half, var_rows, lanes), BF16),
            dma((2, 2)),
            dma((2, 2)),
            dma((3,)),
            dma((3,)),
            dma((2,)),
            dma((2,)),
            dma((2,)),
            dma((2,)),
            dma((2,)),
            dma((2,)),
            dma((2,)),
            dma((2,)),
            dma,
            dma,
            dma,
            dma,
            dma,
            dma,
            dma,
            dma,
            dma,
            dma,
            dma,
            dma,
            dma,
            dma,
            dma,
            dma,
            dma((len(operands),)),
            pltpu.SemaphoreType.REGULAR((2,)),
        ],
        compiler_params=pltpu.CompilerParams(
            collective_id=0, has_side_effects=True, vmem_limit_bytes=40_000_000
        ),
    )(*(pltpu.with_memory_space_constraint(x, pltpu.HBM) for x in operands))
    outs = pl.pallas_call(
        hand_over,
        out_shape=[jax.ShapeDtypeStruct(x.shape, x.dtype) for x in outs],
        in_specs=[pl.BlockSpec(memory_space=pltpu.VMEM)] * len(outs),
        out_specs=[pl.BlockSpec(memory_space=pltpu.HBM)] * len(outs),
        scratch_shapes=[dma((len(outs),))],
        compiler_params=pltpu.CompilerParams(vmem_limit_bytes=20_000_000),
    )(*outs)
    grad_states, grad_query, grad_key, grad_value, grad_wo, grad_dec = outs
    return (
        grad_states[None],
        grad_query[None],
        grad_key[None],
        grad_value[None],
        grad_wo,
        grad_dec,
    )


def solution(mesh):
    banded = P("ens", "space", None)
    in_specs = (
        banded,
        banded,
        banded,
        banded,
        P(),
        P(),
        P(None, "space"),
        P("space"),
        P(),
        P(None, "space"),
        P(None, "space"),
        P(None, "space"),
    )
    out_specs = (banded, banded, banded, banded, P("space", None), P())
    return jax.shard_map(
        per_device, mesh=mesh, in_specs=in_specs, out_specs=out_specs, check_vma=False
    )
```

```python
import functools
import math

import jax
import jax.numpy as jnp
from jax import lax
from jax.experimental import pallas as pl
from jax.experimental.pallas import tpu as pltpu
from jax.sharding import PartitionSpec as P

HEAD_DIM = 64
BLOCK = 128
INNER = 4
LANES = 128
SMOOTH_SQUARE = 0.0625
MASKED_SCORE = -1e30
F32 = jnp.float32
BF16 = jnp.bfloat16
NT = (((1,), (1,)), ((), ()))
TN = (((0,), (0,)), ((), ()))


def smooth_slope(diff_value):
    return diff_value * lax.rsqrt(diff_value * diff_value + SMOOTH_SQUARE)


def dot(a, b, dims=(((1,), (0,)), ((), ()))):
    return lax.dot_general(a, b, dims, preferred_element_type=F32)


def kernel(
    n_e,
    n_s,
    states_hbm,
    q_hbm,
    k_hbm,
    v_hbm,
    ow_hbm,
    dec_hbm,
    target_hbm,
    area_hbm,
    var_hbm,
    edges_hbm,
    ew_hbm,
    win_hbm,
    gs_ref,
    gq_ref,
    gk_ref,
    gv_ref,
    gwo_ref,
    gdec_ref,
    states_ref,
    q_ref,
    k_ref,
    v_ref,
    ow_ref,
    dec_ref,
    target_ref,
    area_ref,
    var_ref,
    edges_ref,
    ew_ref,
    win_ref,
    decp,
    mix,
    wt,
    kh,
    text,
    gp,
    qsend,
    qrecv,
    qs,
    prob,
    ao,
    go,
    kmid,
    vmid,
    gsc,
    qn,
    rows_own,
    rows_near,
    slab,
    stat,
    stat_near,
    go_near,
    csend,
    cpair,
    cmid,
    crecv,
    dsend,
    dpair,
    dmid,
    drecv,
    zsend,
    zrecv,
    fsend,
    frecv,
    agsend,
    dall,
    kv_s,
    kv_r,
    t_s,
    t_r,
    q_s,
    q_r,
    qn_s,
    qn_r,
    n_s_sem,
    n_r_sem,
    st_s,
    st_r,
    c_s,
    c_r,
    d_s,
    d_r,
    a_s,
    a_r,
    z_s,
    z_r,
    f_s,
    f_r,
    pd_s,
    pd_r,
    pc_s,
    pc_r,
    pa_s,
    pa_r,
    load_sem,
    hello_sem,
):
    e = lax.axis_index("ens")
    s = lax.axis_index("space")
    inner = math.gcd(n_s, INNER)
    outer = n_s // inner
    group = n_e * inner
    ring, seat = lax.div(s, inner), lax.rem(s, inner)
    pair = math.gcd(inner, 2)
    rows_in = inner // pair
    half = group // pair
    place, parity = lax.div(seat, pair), lax.rem(seat, pair)
    mine = e * rows_in + place
    spots = n_e * outer
    everyone = half * outer
    flat = drecv.shape[0] == everyone
    seat_all = mine * outer + ring
    nodes, width = states_ref.shape
    att = q_ref.shape[1]
    pairs = att // LANES
    n_var = dec_ref.shape[0]
    points = target_ref.shape[1]
    scale = 1.0 / math.sqrt(HEAD_DIM)
    has_left = s > 0
    has_right = s < n_s - 1
    sides = ((0, -1, has_left), (1, 1, has_right))
    rings = ((0, -1, ring > 0), (1, 1, ring < outer - 1))

    def remote(src, dst, send_sem, recv_sem, ens, space):
        return pltpu.make_async_remote_copy(
            src_ref=src,
            dst_ref=dst,
            send_sem=send_sem,
            recv_sem=recv_sem,
            device_id=(ens, space),
            device_id_type=pl.DeviceIdType.MESH,
        )

    def received(dst, sem):
        remote(dst, dst, sem, sem, e, s).wait_recv()

    def sent(src, sem):
        remote(src, src, sem, sem, e, s).wait_send()

    loads = {}
    for i, (name, source, held) in enumerate(
        (
            ("states", states_hbm, states_ref),
            ("dec", dec_hbm, dec_ref),
            ("edges", edges_hbm, edges_ref),
            ("ew", ew_hbm, ew_ref),
            ("k", k_hbm, k_ref),
            ("v", v_hbm, v_ref),
            ("target", target_hbm, target_ref),
            ("area", area_hbm, area_ref),
            ("var", var_hbm, var_ref),
            ("win", win_hbm, win_ref),
            ("ow", ow_hbm, ow_ref),
            ("q", q_hbm, q_ref),
        )
    ):
        loads[name] = pltpu.make_async_copy(source, held, load_sem.at[i])

    def loaded(*wanted):
        for name in wanted:
            loads[name].wait()

    for load in loads.values():
        load.start()

    barrier = pltpu.get_barrier_semaphore()

    def under(present, action):
        if present is None:
            action()
        else:
            pl.when(present)(action)

    def signal(semaphore, ens, space):
        pl.semaphore_signal(
            semaphore,
            inc=1,
            device_id=(ens, space),
            device_id_type=pl.DeviceIdType.MESH,
        )

    near = [
        (lax.rem(e + r, n_e), s + shift, present)
        for shift, present in ((-1, has_left), (1, has_right), (0, None))
        for r in range(n_e)
        if r or shift
    ] + [(e, s + shift * inner, present) for _, shift, present in rings if inner > 1]

    for ens, space, present in near:
        under(present, functools.partial(signal, barrier, ens, space))

    def hello():
        for side, shift, present in rings:
            under(
                present,
                functools.partial(signal, hello_sem.at[1 - side], e, s + shift * inner),
            )

    def hello_wait():
        for side, _, present in rings:
            under(present, functools.partial(pl.semaphore_wait, hello_sem.at[side], 1))

    for slot, _, present in sides:

        @pl.when(jnp.logical_not(present))
        def _():
            kh[slot] = jnp.zeros(kh.shape[1:], BF16)
            text[2 * slot] = jnp.zeros(text.shape[1:], BF16)
            qrecv[slot] = jnp.zeros(qrecv.shape[1:], BF16)
            qn[slot] = jnp.zeros(qn.shape[1:], BF16)
            rows_near[slot] = jnp.zeros(rows_near.shape[1:], BF16)
            stat_near[slot] = jnp.zeros(stat_near.shape[1:], F32)

    decp[...] = jnp.zeros(decp.shape, BF16)
    loaded("states", "dec")
    decp[0:n_var, :] = dec_ref[...]
    text[1, e] = dot(decp[...], states_ref[...], NT).astype(BF16)
    peers = sum(1 if present is None else present.astype(jnp.int32) for _, _, present in near)
    pl.semaphore_wait(barrier, peers)

    for r in range(n_e):
        ens = lax.rem(e + r, n_e)
        for shift, present in ((-1, has_left), (1, has_right), (0, None)):
            if r or shift:
                out = remote(
                    text.at[1, e],
                    text.at[1 - shift, e],
                    t_s.at[1 + shift],
                    t_r.at[1 - shift],
                    ens,
                    s + shift,
                )
                under(present, out.start)
    if outer > 1:
        hello()

    def kv_copy(slot, shift, item):
        return remote(
            k_ref if item == 0 else v_ref,
            kh.at[1 - slot, item],
            kv_s.at[slot, item],
            kv_r.at[1 - slot, item],
            e,
            s + shift,
        )

    def to_sides(src, dst, s_sem, r_sem, when=(None, None)):
        for slot, shift, present in sides:
            if when[slot] is not False:
                out = remote(
                    src, dst.at[1 - slot], s_sem.at[slot], r_sem.at[1 - slot], e, s + shift
                )
                under(present if when[slot] is None else present & when[slot], out.start)

    last_seat = seat == inner - 1

    def start_kv(item, when=(None, None)):
        for slot, shift, present in sides:
            if when[slot] is not False:
                shown = present if when[slot] is None else present & when[slot]
                under(shown, kv_copy(slot, shift, item).start)

    loaded("k", "v")
    start_kv(0, (None, jnp.logical_not(last_seat)))

    loaded("edges", "ew")
    first = (s - 1) * nodes
    chunk = nodes
    for part in range(3):
        node_ids = first + part * chunk + lax.broadcasted_iota(jnp.int32, (chunk, points), 0)
        total = jnp.zeros((chunk, points), F32)
        for slot in range(edges_ref.shape[0]):
            total = total + jnp.where(
                node_ids == edges_ref[slot : slot + 1, :], ew_ref[slot : slot + 1, :], 0.0
            )
        wt[part * chunk : (part + 1) * chunk, :] = total.astype(BF16)

    loaded("target", "area", "var", "win", "q", "ow")
    mix[...] = dot(decp[...], ow_ref[...], NT).astype(BF16)

    if n_e > 1:
        received(text.at[1, pl.ds(0, n_e - 1)], t_r.at[1])
    for slot, _, present in sides:
        under(present, functools.partial(received, text.at[2 * slot], t_r.at[2 * slot]))
    start_kv(0, (False, last_seat))
    if outer > 1:
        hello_wait()
        hello()

    def predictions(member):
        cat = jnp.concatenate([text[i, member] for i in range(3)], axis=1)
        return dot(cat, wt[...])[0:n_var].astype(BF16).astype(F32)

    own_pred = predictions(e)
    slopes = smooth_slope(own_pred - target_ref[...])
    pair_sum = jnp.zeros_like(own_pred)
    for r in range(1, n_e):
        pair_sum = pair_sum + smooth_slope(own_pred - predictions(lax.rem(e + r, n_e)))
    slopes = slopes - pair_sum / (n_e - 1)
    square = (n_var, n_var)
    diagonal = lax.broadcasted_iota(jnp.int32, square, 0) == lax.broadcasted_iota(
        jnp.int32, square, 1
    )
    var_column = jnp.sum(jnp.where(diagonal, var_ref[...], 0.0), axis=1, keepdims=True)
    gp[...] = jnp.zeros(gp.shape, BF16)
    gp[0:n_var, :] = (area_ref[...] * var_column * slopes).astype(BF16)
    q_ext = dot(gp[...], wt[...], NT)
    qsend[0] = q_ext[:, 0:nodes].astype(BF16)
    qsend[1] = q_ext[:, 2 * nodes :].astype(BF16)

    for slot, shift, present in sides:
        out = remote(
            qsend.at[slot], qrecv.at[1 - slot], q_s.at[slot], q_r.at[1 - slot], e, s + shift
        )
        under(present, out.start)
    start_kv(1, (None, jnp.logical_not(last_seat)))

    blocks = win_ref.shape[0]
    key_place = first + lax.broadcasted_iota(jnp.int32, (1, 3 * nodes), 1)
    inside_rows = [
        (key_place >= win_ref[b : b + 1, 0:1]) & (key_place < win_ref[b : b + 1, 1:2])
        for b in range(blocks)
    ]
    heads_per = LANES // HEAD_DIM
    lane_head = lax.broadcasted_iota(jnp.int32, (nodes, LANES), 1) // HEAD_DIM

    def split_heads(x):
        x = x.astype(F32)
        return jnp.concatenate(
            [jnp.where(lane_head == h, x, 0.0).astype(BF16) for h in range(heads_per)], axis=0
        )

    def merge_heads(x):
        out = x[0:nodes]
        for h in range(1, heads_per):
            out = jnp.where(lane_head == h, x[h * nodes : (h + 1) * nodes], out)
        return out

    def extended(item, own_ref, columns):
        return jnp.concatenate(
            [kh[0, item, :, columns], own_ref[:, columns], kh[1, item, :, columns]], axis=0
        )

    def columns_of(p):
        return slice(p * LANES, (p + 1) * LANES)

    for p in range(pairs):
        qs[p] = split_heads(q_ref[:, columns_of(p)].astype(F32) * scale)

    def arrived(item):
        for slot, _, present in sides:
            under(present, functools.partial(received, kh.at[slot, item], kv_r.at[slot, item]))

    if outer > 2:
        hello_wait()
        hello()
    for slot, _, present in sides:
        under(present, functools.partial(received, qrecv.at[slot], q_r.at[slot]))
    start_kv(1, (False, last_seat))
    to_sides(q_ref, qn, qn_s, qn_r, (False, last_seat))
    q_own = q_ext[:, nodes : 2 * nodes] + qrecv[0].astype(F32) + qrecv[1].astype(F32)
    q_rows = q_own.T.astype(BF16)
    rows_own[...] = q_rows
    dec_term = dot(q_own.astype(BF16), states_ref[...])
    var_rows, lanes = dsend.shape[2:]
    for c in range(group):
        dsend[c // half, c % half] = dec_term[0:var_rows, c * lanes : (c + 1) * lanes].astype(BF16)

    def pair_start(source, target, s_sem, r_sem):
        if pair > 1:
            remote(source, target, s_sem, r_sem, e, s + 1 - 2 * parity).start()

    def plane_start(source, target, s_sem, r_sem):
        @pl.loop(1, half)
        def _(i):
            to = lax.rem(mine + i, half)
            ens, row = lax.div(to, rows_in), lax.rem(to, rows_in)
            remote(
                source if source is agsend else source.at[to],
                target,
                s_sem,
                r_sem,
                ens,
                ring * inner + row * pair + parity,
            ).start()

    pair_start(dsend.at[1 - parity], dpair, pd_s, pd_r)
    to_sides(rows_own, rows_near, n_s_sem, n_r_sem)
    go[...] = dot(q_rows, mix[...]).astype(BF16)
    if outer > 3:
        hello_wait()
        hello()
    if pair > 1:
        received(dpair, pd_r)
        dmid[...] = (dsend[parity].astype(F32) + dpair[...].astype(F32)).astype(BF16)
    else:
        dmid[...] = dsend[parity]
    if outer > 1:
        hello_wait()
    for _ in range(outer - 4):
        hello()
        hello_wait()
    if flat:
        piece = drecv.shape[1]

        def all_start(source_of, target, s_sem, r_sem):
            for far in range(outer):
                around = lax.rem(ring + far, outer)
                for across in range(n_e):
                    ens = lax.rem(e + across, n_e)
                    for along in range(rows_in):
                        if far or across or along:
                            row = lax.rem(place + along, rows_in)
                            remote(
                                source_of(ens * rows_in + row, row, around),
                                target,
                                s_sem,
                                r_sem,
                                ens,
                                around * inner + row * pair + parity,
                            ).start()

        def piece_rows(around):
            return pl.ds(pl.multiple_of(around * piece, piece), piece)

        all_start(
            lambda member, row, around: dmid.at[member, piece_rows(around)],
            drecv.at[seat_all],
            d_s,
            d_r,
        )
        drecv[seat_all] = dmid[mine, piece_rows(ring)]
    else:
        plane_start(dmid, drecv.at[mine], d_s, d_r)
        drecv[mine] = dmid[mine]
    arrived(0)
    heads_rows = heads_per * nodes
    stat_lane = lax.broadcasted_iota(jnp.int32, (heads_rows, LANES), 1)

    def put_stat(held, at, column):
        return jnp.where(stat_lane == at, column, held)

    stats = jnp.zeros((heads_rows, LANES), F32)
    for bound in range(2):
        edge = jnp.concatenate(
            [
                jnp.broadcast_to(
                    win_ref[i % blocks : i % blocks + 1, bound : bound + 1].astype(F32),
                    (BLOCK, 1),
                )
                for i in range(blocks * heads_per)
            ],
            axis=0,
        )
        stats = put_stat(stats, 3 * pairs + bound, edge)
    for p in range(pairs):
        columns = columns_of(p)
        scores = dot(qs[p], extended(0, k_ref, columns), NT)
        if blocks == 1:
            scores = jnp.where(inside_rows[0], scores, MASKED_SCORE)
        else:
            scores = jnp.concatenate(
                [
                    jnp.where(
                        inside_rows[i % blocks],
                        scores[i * BLOCK : (i + 1) * BLOCK],
                        MASKED_SCORE,
                    )
                    for i in range(blocks * heads_per)
                ],
                axis=0,
            )
        row_max = jnp.max(scores, axis=-1, keepdims=True)
        exponent = jnp.exp(scores - row_max)
        inverse = 1.0 / jnp.sum(exponent, axis=-1, keepdims=True)
        prob[p] = exponent * inverse
        stats = put_stat(stats, p, row_max)
        stats = put_stat(stats, pairs + p, inverse)

    slab[...] = stats
    arrived(1)
    for p in range(pairs):
        columns = columns_of(p)
        ao[:, columns] = merge_heads(
            dot(prob[p].astype(BF16), extended(1, v_ref, columns))
        ).astype(BF16)
    wo_rows = fsend.shape[1]
    wo_term = dot(ao[...], q_rows, TN)
    for c in range(inner):
        for o in range(outer):
            top = (o * inner + c) * wo_rows
            csend[c % pair, c // pair, o * wo_rows : (o + 1) * wo_rows] = wo_term[
                top : top + wo_rows
            ].astype(BF16)
    pair_start(csend.at[1 - parity], cpair, pc_s, pc_r)
    def wo_across():
        if pair > 1:
            received(cpair, pc_r)
            cmid[...] = (csend[parity].astype(F32) + cpair[...].astype(F32)).astype(BF16)
        else:
            cmid[...] = csend[parity]

        @pl.loop(1, rows_in)
        def _(i):
            to = lax.rem(place + i, rows_in)
            remote(
                cmid.at[to], crecv.at[place], c_s, c_r, e, ring * inner + to * pair + parity
            ).start()

        crecv[place] = cmid[place]

    def gather_flat():
        received(drecv.at[pl.ds(0, everyone - 1)], d_r)
        dec_sum = jnp.sum(drecv[...].astype(F32), axis=0).astype(BF16)
        agsend[...] = dec_sum
        dall[parity, mine, piece_rows(ring)] = dec_sum
        all_start(
            lambda member, row, around: agsend,
            dall.at[parity, mine, piece_rows(ring)],
            a_s,
            a_r,
        )

    def wo_around():
        if rows_in > 1:
            received(crecv.at[pl.ds(0, rows_in - 1)], c_r)
        wo_plane = jnp.sum(crecv[...].astype(F32), axis=0).astype(BF16)
        for o in range(outer):
            fsend[o] = wo_plane[o * wo_rows : (o + 1) * wo_rows]
        spot = e * outer + ring
        frecv[spot] = fsend[ring]

        @pl.loop(1, spots)
        def _(i):
            to = lax.rem(spot + i, spots)
            ens, around = lax.div(to, outer), lax.rem(to, outer)
            remote(fsend.at[around], frecv.at[spot], f_s, f_r, ens, around * inner + seat).start()

    def gather_planes():
        received(drecv.at[pl.ds(0, half - 1)], d_r)
        dec_plane = jnp.sum(drecv[...].astype(F32), axis=0).astype(BF16)
        zsend[...] = dec_plane
        zrecv[ring] = dec_plane

        @pl.loop(1, outer)
        def _(i):
            to = lax.rem(ring + i, outer)
            remote(zsend, zrecv.at[ring], z_s, z_r, e, to * inner + seat).start()

        wo_around()
        if outer > 1:
            received(zrecv.at[pl.ds(0, outer - 1)], z_r)
        dec_sum = jnp.sum(zrecv[...].astype(F32), axis=0).astype(BF16)
        agsend[...] = dec_sum
        dall[parity, mine] = dec_sum
        plane_start(agsend, dall.at[parity, mine], a_s, a_r)

    stats = slab[...]
    for p in range(pairs):
        columns = columns_of(p)
        attn_prob = prob[p]
        grad_prob = dot(split_heads(go[:, columns]), extended(1, v_ref, columns), NT)
        row_delta = jnp.sum(attn_prob * grad_prob, axis=-1, keepdims=True)
        gsc[p] = (attn_prob * (grad_prob - row_delta)).astype(BF16)
        stats = put_stat(stats, 2 * pairs + p, row_delta)
    stat[...] = stats.T[0 : stat.shape[0]]
    wo_across()
    to_sides(stat, stat_near, st_s, st_r)
    to_sides(q_ref, qn, qn_s, qn_r, (None, jnp.logical_not(last_seat)))
    for p in range(pairs):
        columns = columns_of(p)
        middle = slice(nodes, 2 * nodes)
        grads = split_heads(go[:, columns])
        kmid[:, columns] = dot(gsc[p, :, middle], qs[p], TN)
        vmid[:, columns] = dot(prob[p, :, middle].astype(BF16), grads, TN)
        gq_ref[:, columns] = (
            merge_heads(dot(gsc[p], extended(0, k_ref, columns))) * scale
        ).astype(BF16)

    gs_ref[...] = dot(q_rows, decp[...]).astype(BF16)
    if flat:
        gather_flat()
        wo_around()
    else:
        gather_planes()
    for slot, _, present in sides:
        under(present, functools.partial(received, rows_near.at[slot], n_r_sem.at[slot]))
        under(present, functools.partial(received, qn.at[slot], qn_r.at[slot]))
        under(present, functools.partial(received, stat_near.at[slot], st_r.at[slot]))
    for slot in range(2):
        go_near[slot] = dot(rows_near[slot], mix[...]).astype(BF16)
    key_column = (
        s * nodes + lax.broadcasted_iota(jnp.int32, (nodes, 2 * heads_rows), 0)
    ).astype(F32)

    def near_stat(at):
        return jnp.concatenate([stat_near[i, at : at + 1, :] for i in range(2)], axis=1)

    allowed = (key_column >= near_stat(3 * pairs)) & (key_column < near_stat(3 * pairs + 1))
    for p in range(pairs):
        columns = columns_of(p)
        q_near = jnp.concatenate(
            [split_heads(qn[i, :, columns].astype(F32) * scale) for i in range(2)], axis=0
        )
        g_near = jnp.concatenate([split_heads(go_near[i, :, columns]) for i in range(2)], axis=0)
        scores = dot(k_ref[:, columns], q_near, NT)
        near_prob = jnp.exp(
            jnp.where(allowed, scores - near_stat(p), MASKED_SCORE)
        ) * near_stat(pairs + p)
        near_grad = dot(v_ref[:, columns], g_near, NT)
        near_scores = near_prob * (near_grad - near_stat(2 * pairs + p))
        gv_ref[:, columns] = (
            vmid[:, columns] + dot(near_prob.astype(BF16), g_near)
        ).astype(BF16)
        gk_ref[:, columns] = (
            kmid[:, columns] + dot(near_scores.astype(BF16), q_near)
        ).astype(BF16)

    parts = drecv.shape[0]
    received(drecv.at[pl.ds(0, parts - 1)], a_r)
    pair_start(dall.at[parity], dall.at[parity], pa_s, pa_r)
    if frecv.shape[0] > 1:
        received(frecv.at[pl.ds(0, frecv.shape[0] - 1)], f_r)
    wo_sum = jnp.sum(frecv[...].astype(F32), axis=0)
    gwo_ref[...] = dot(wo_sum.astype(BF16), decp[...])

    for slot, shift, present in sides:

        def drain():
            for _ in range(n_e):
                sent(text.at[1, 0], t_s.at[1 + shift])
            for item in range(2):
                sent(kh.at[slot, item], kv_s.at[slot, item])
            sent(qsend.at[slot], q_s.at[slot])
            sent(qn.at[slot], qn_s.at[slot])
            sent(rows_own, n_s_sem.at[slot])
            sent(stat, st_s.at[slot])

        under(present, drain)
    if n_e > 1:
        sent(text.at[1, pl.ds(0, n_e - 1)], t_s.at[1])
    if pair > 1:
        sent(dpair, pd_s)
        sent(cpair, pc_s)
    sent(drecv.at[pl.ds(0, parts - 1)], d_s)
    if rows_in > 1:
        sent(crecv.at[pl.ds(0, rows_in - 1)], c_s)
    if not flat and outer > 1:
        sent(zrecv.at[pl.ds(0, outer - 1)], z_s)
    if frecv.shape[0] > 1:
        sent(frecv.at[pl.ds(0, frecv.shape[0] - 1)], f_s)
    sent(drecv.at[pl.ds(0, parts - 1)], a_s)
    if pair > 1:
        received(dpair, pa_r)
    for c in range(group):
        gdec_ref[:, c * lanes : (c + 1) * lanes] = dall[c // half, c % half].astype(F32)[0:n_var]
    if pair > 1:
        sent(dpair, pa_s)


def hand_over(*refs):
    count = (len(refs) - 1) // 2
    sems = refs[-1]
    copies = [
        pltpu.make_async_copy(refs[i], refs[count + i], sems.at[i]) for i in range(count)
    ]
    for copy in copies:
        copy.start()
    for copy in copies:
        copy.wait()


def per_device(
    node_states,
    query,
    key,
    value,
    out_weight,
    dec_weight,
    target,
    area_weight,
    var_weight,
    edges,
    edge_weight,
    windows,
):
    n_e, n_s = lax.axis_size("ens"), lax.axis_size("space")
    inner = math.gcd(n_s, INNER)
    outer, group = n_s // inner, n_e * inner
    pair = math.gcd(inner, 2)
    half = group // pair
    nodes, width = node_states.shape[1:]
    att = query.shape[2]
    n_var, points = target.shape
    pairs = att // LANES
    var_pad = -(-n_var // LANES) * LANES
    flat = var_pad % (16 * outer) == 0
    var_rows = var_pad if flat else -(-n_var // 16) * 16
    piece = var_rows // outer if flat else var_rows
    lanes = width // group
    wo_rows = att // n_s
    span = 3 * nodes
    heads_per = LANES // HEAD_DIM
    stat_rows = -(-(3 * pairs + 2) // 8) * 8
    dma = pltpu.SemaphoreType.DMA
    operands = (
        node_states[0],
        query[0],
        key[0],
        value[0],
        out_weight,
        dec_weight,
        target,
        area_weight[None, :],
        var_weight[None, :],
        edges,
        edge_weight,
        windows.T,
    )
    outs = pl.pallas_call(
        functools.partial(kernel, n_e, n_s),
        out_shape=(
            pltpu.VMEM((nodes, width), BF16),
            pltpu.VMEM((nodes, att), BF16),
            pltpu.VMEM((nodes, att), BF16),
            pltpu.VMEM((nodes, att), BF16),
            pltpu.VMEM((wo_rows, width), F32),
            pltpu.VMEM((n_var, width), F32),
        ),
        in_specs=[pl.BlockSpec(memory_space=pltpu.HBM)] * len(operands),
        out_specs=[pl.BlockSpec(memory_space=pltpu.VMEM)] * 6,
        scratch_shapes=[pltpu.VMEM(x.shape, x.dtype) for x in operands]
        + [
            pltpu.VMEM((var_pad, width), BF16),
            pltpu.VMEM((var_pad, att), BF16),
            pltpu.VMEM((span, points), BF16),
            pltpu.VMEM((2, 2, nodes, att), BF16),
            pltpu.VMEM((3, n_e, var_pad, nodes), BF16),
            pltpu.VMEM((var_pad, points), BF16),
            pltpu.VMEM((2, var_pad, nodes), BF16),
            pltpu.VMEM((2, var_pad, nodes), BF16),
            pltpu.VMEM((pairs, heads_per * nodes, LANES), BF16),
            pltpu.VMEM((pairs, heads_per * nodes, span), F32),
            pltpu.VMEM((nodes, att), BF16),
            pltpu.VMEM((nodes, att), BF16),
            pltpu.VMEM((nodes, att), F32),
            pltpu.VMEM((nodes, att), F32),
            pltpu.VMEM((pairs, heads_per * nodes, span), BF16),
            pltpu.VMEM((2, nodes, att), BF16),
            pltpu.VMEM((nodes, var_pad), BF16),
            pltpu.VMEM((2, nodes, var_pad), BF16),
            pltpu.VMEM((heads_per * nodes, LANES), F32),
            pltpu.VMEM((stat_rows, heads_per * nodes), F32),
            pltpu.VMEM((2, stat_rows, heads_per * nodes), F32),
            pltpu.VMEM((2, nodes, att), BF16),
            pltpu.VMEM((pair, inner // pair, outer * wo_rows, var_pad), BF16),
            pltpu.VMEM((inner // pair, outer * wo_rows, var_pad), BF16),
            pltpu.VMEM((inner // pair, outer * wo_rows, var_pad), BF16),
            pltpu.VMEM((inner // pair, outer * wo_rows, var_pad), BF16),
            pltpu.VMEM((pair, half, var_rows, lanes), BF16),
            pltpu.VMEM((half, var_rows, lanes), BF16),
            pltpu.VMEM((half, var_rows, lanes), BF16),
            pltpu.VMEM((half * outer if flat else half, piece, lanes), BF16),
            pltpu.VMEM((var_rows, lanes), BF16),
            pltpu.VMEM((outer, var_rows, lanes), BF16),
            pltpu.VMEM((outer, wo_rows, var_pad), BF16),
            pltpu.VMEM((n_e * outer, wo_rows, var_pad), BF16),
            pltpu.VMEM((piece, lanes), BF16),
            pltpu.VMEM((pair, half, var_rows, lanes), BF16),
            dma((2, 2)),
            dma((2, 2)),
            dma((3,)),
            dma((3,)),
            dma((2,)),
            dma((2,)),
            dma((2,)),
            dma((2,)),
            dma((2,)),
            dma((2,)),
            dma((2,)),
            dma((2,)),
            dma,
            dma,
            dma,
            dma,
            dma,
            dma,
            dma,
            dma,
            dma,
            dma,
            dma,
            dma,
            dma,
            dma,
            dma,
            dma,
            dma((len(operands),)),
            pltpu.SemaphoreType.REGULAR((2,)),
        ],
        compiler_params=pltpu.CompilerParams(
            collective_id=0, has_side_effects=True, vmem_limit_bytes=40_000_000
        ),
    )(*(pltpu.with_memory_space_constraint(x, pltpu.HBM) for x in operands))
    outs = pl.pallas_call(
        hand_over,
        out_shape=[jax.ShapeDtypeStruct(x.shape, x.dtype) for x in outs],
        in_specs=[pl.BlockSpec(memory_space=pltpu.VMEM)] * len(outs),
        out_specs=[pl.BlockSpec(memory_space=pltpu.HBM)] * len(outs),
        scratch_shapes=[dma((len(outs),))],
        compiler_params=pltpu.CompilerParams(vmem_limit_bytes=20_000_000),
    )(*outs)
    grad_states, grad_query, grad_key, grad_value, grad_wo, grad_dec = outs
    return (
        grad_states[None],
        grad_query[None],
        grad_key[None],
        grad_value[None],
        grad_wo,
        grad_dec,
    )


def solution(mesh):
    banded = P("ens", "space", None)
    in_specs = (
        banded,
        banded,
        banded,
        banded,
        P(),
        P(),
        P(None, "space"),
        P("space"),
        P(),
        P(None, "space"),
        P(None, "space"),
        P(None, "space"),
    )
    out_specs = (banded, banded, banded, banded, P("space", None), P())
    return jax.shard_map(
        per_device, mesh=mesh, in_specs=in_specs, out_specs=out_specs, check_vma=False
    )
```
